32 devices in a mesh: inline: 4 (over y, core), xline: 8 (over z, x).
Axes of the slice: x: 2, y: 2, z: 4, core: 2. Of those that a mesh axis runs over, the one named last changes fastest.
Arguments:
- records: bfloat16 [2, 4, 8, 8, 8192], P(None, 'inline', 'xline'), may hold values from -6 to 6
- beam_count: int32 [4, 8], P('inline', 'xline'), may hold values from 1 to 8, 40 in all within a row
- owner_list: int32 [2560, 1], P(('inline', 'xline')), may hold values from 0 to 7; in each aligned block of 80 rows (0 to 79, 80 to 159, ...) at most 20 rows name the same one
- block_list: int32 [2560, 1], P(('inline', 'xline')), may hold values from 0 to 127
- travel_table: float32 [1024, 64, 128], P('xline'), may hold values from 1 to 126
- amp_table: float32 [1024, 64, 128], P('xline'), may hold values from -6 to 6
Outputs:
- image: float32 [4, 8, 128], P('inline', 'xline')
The draws below stay inside these ranges and needn't reach their ends.
Inputs may be any that keep to these rules, and one draw needn't show every extreme that they name: `owner_list`: the 80 rows of one tile name each owner at most 20 times, a bound that some block reaches. `beam_count`: some tile of every inline row has all 8 beams live.
All inputs are finite; a program needn't handle non-finite values. No bound on the sum of `beam_count` on one device may be relied on, other than what follows from the above.
Results may differ from the reference program's by a relative error of at most 0.0026.
Values may be sent and summed in bfloat16 or wider, within the bound.
No kernel may reach another device: no remote copies, remote signals or barrier semaphores. Data moves between devices by JAX's collectives and lax.ppermute only.
A program may use at most 64 MiB of HBM per device.

```python
import math
import jax
import jax.numpy as jnp
import numpy as np
from jax import lax

NS = 128
NP = 64
PTS = 128
BEAM_DEV = 8
SHOTS = 2
BLK_DEV = 128
REQ = 80
CAP = 20
NBLK = 1024
N_INLINE = 4
N_XLINE = 8


def with_ends(drawn, stream_key, smallest, high):
    place = [jax.random.randint(jax.random.fold_in(stream_key, axis), (), 0, length) for axis, length in enumerate(drawn.shape)]
    widest = drawn.shape.index(max(drawn.shape))
    neighbour = place[:widest] + [(place[widest] + 1) % drawn.shape[widest]] + place[widest + 1:]
    return drawn.at[tuple(place)].set(smallest).at[tuple(neighbour)].set(high)


def block_scale(key, shape, cuts, least, largest):
    factor_of = 1.0
    for dim, parts in cuts:
        steps = jax.random.uniform(jax.random.fold_in(jax.random.fold_in(key, 6), dim), (parts,), jnp.float32, least / len(cuts), largest / len(cuts))
        factor_of = factor_of * jnp.repeat(jnp.exp(steps), shape[dim] // parts).reshape((-1,) + (1,) * (len(shape) - 1 - dim))
    return factor_of


def profile(count, total, bound, lean):
    weights = [(1 << 20) // math.isqrt(grade ** lean) + 1 for grade in range(2, count + 1)]
    rest, holding = total - bound - (count - 1), [1] * (count - 1)
    while rest > 0:
        free = [i for i in range(count - 1) if holding[i] < bound]
        whole, left = sum([weights[i] for i in free]), rest
        for i in free:
            extra = min(bound - holding[i], max(1, left * weights[i] // whole), rest)
            holding[i] = holding[i] + extra
            rest = rest - extra
    return np.array([bound] + holding)


def uneven_parts(key, number_of, total, bound, lean):
    if number_of == 2:
        one = jax.random.randint(key, (), max(1, total - bound), min(bound, total - 1) + 1)
        return jnp.stack([one, total - one])
    sizes = jnp.asarray(profile(number_of, total, bound, lean), jnp.int32)
    twos = (number_of - 1) // 2
    donor, taker = sizes[1:1 + 2 * twos:2], sizes[2:2 + 2 * twos:2]
    margin = jnp.minimum(donor - 1, bound - taker)
    moved = jax.random.randint(jax.random.fold_in(key, 1), (twos,), 0, 1 << 20) % (margin + 1)
    sizes = sizes.at[1:1 + 2 * twos:2].set(donor - moved).at[2:2 + 2 * twos:2].set(taker + moved)
    return sizes[jax.random.permutation(jax.random.fold_in(key, 2), number_of)]


def deal_out(stream_key, own, number, rows, amount, top, limit, slope):
    sequence = jax.random.permutation(stream_key, amount)
    heavy_load, common = load_shares(amount, rows * top, limit, slope, True), load_shares(amount, rows * top, limit, slope, False)
    places = jnp.arange(amount)

    def named(tallies, turn):
        used = int((tallies > 0).sum())
        fixed = max(1, used // 4)
        shifted = fixed + (places - fixed + turn * (used - fixed)) % max(1, amount - fixed)
        return jnp.zeros((amount,), jnp.int32).at[sequence[jnp.where(places < fixed, places, shifted)]].set(jnp.asarray(tallies, jnp.int32))

    tallies = jnp.where(number % 4 == 0, named(heavy_load, number // 4), named(common, number - number // 4 - 1))
    mixed = jax.random.permutation(jax.random.fold_in(own, 3), amount)
    giver, taker = mixed[0:amount // 2 * 2:2], mixed[1:amount // 2 * 2:2]
    room = jnp.minimum(tallies[giver] - 1, limit - tallies[taker]) // 2
    room = jnp.where((giver == sequence[0]) | (taker == sequence[0]) | (tallies[taker] == 0), 0, jnp.maximum(room, 0))
    shifted = jax.random.randint(jax.random.fold_in(own, 4), (amount // 2,), 0, 1 << 20) % (room + 1)
    tallies = tallies.at[giver].add(-shifted).at[taker].add(shifted)
    items = jnp.searchsorted(jnp.cumsum(tallies), jnp.arange(rows * top), side="right").astype(jnp.int32)
    grid = items.reshape(top, rows).T
    grid = grid[jax.random.permutation(jax.random.fold_in(own, 1), rows)]
    turn = jax.random.randint(jax.random.fold_in(own, 2), (rows, 1), 0, top)
    return jnp.take_along_axis(grid, (jnp.arange(top)[None, :] + turn) % top, axis=1)


def load_shares(number_of, total, most, slope, full):
    portions = [(1 << 20) // math.isqrt(standing ** slope) + 1 for standing in range(1, number_of + 1)]
    largest = most if full else min(most, max(-(-total // number_of), total * portions[0] // sum(portions)))
    least = 1 if total - largest >= number_of - 1 else 0
    counts, rest = [largest] + [least] * (number_of - 1), total - largest - least * (number_of - 1)
    while rest > 0:
        movable = [i for i in range(1, number_of) if counts[i] < largest] or [i for i in range(1, number_of) if counts[i] < most]
        pool, budget = sum([portions[i] for i in movable]), rest
        for i in movable:
            addition = min(most - counts[i], max(1, budget * portions[i] // pool), rest)
            counts[i] = counts[i] + addition
            rest = rest - addition
    return np.array(counts)


def normal_values(key, dims, spread, limit, cuts=(), held_as=jnp.bfloat16):
    loudness = block_scale(key, dims, cuts, -0.22, 0.18) if cuts else 1.0
    entries = jax.random.normal(key, dims, jnp.float32) * spread * loudness
    return jnp.minimum(jnp.maximum(entries, -limit), limit).astype(held_as)


def setup_inputs(seed: int = 0) -> dict:
    streams_of = jax.random.split(jax.random.key(seed), 7)
    records = normal_values(streams_of[0], (SHOTS, N_INLINE, N_XLINE, BEAM_DEV, NP * NS), 1.0, 6.0, ((1, 4), (2, 8)))
    beam_count = jax.vmap(lambda own: uneven_parts(own, N_XLINE, N_XLINE * BEAM_DEV * 5 // 8, BEAM_DEV, 2))(jax.random.split(streams_of[1], N_INLINE)).reshape((N_INLINE, N_XLINE)).astype(jnp.int32)
    owner_list_keys = jax.random.split(jax.random.fold_in(streams_of[2], 1), (N_INLINE * N_XLINE * REQ) // REQ)
    owner_list_turns = jax.random.permutation(jax.random.fold_in(streams_of[2], 3), (N_INLINE * N_XLINE * REQ) // REQ)
    owner_list = jax.vmap(lambda own, number: deal_out(jax.random.fold_in(streams_of[2], 2), own, number, REQ, N_XLINE, 1, CAP, 2))(owner_list_keys, owner_list_turns).reshape((N_INLINE * N_XLINE * REQ, 1))
    block_list = with_ends(jax.random.randint(streams_of[3], (N_INLINE * N_XLINE * REQ, 1), 0, BLK_DEV), jax.random.fold_in(streams_of[3], 1), 0, BLK_DEV - 1).astype(jnp.int32)
    travel_table = jnp.clip(1.0 + 125.0 * jax.random.uniform(streams_of[4], (NBLK, NP, PTS), jnp.float32) ** block_scale(streams_of[4], (NBLK, NP, PTS), ((0, 8),), -0.2, 0.2), 1.0, 126.0)
    amp_table = normal_values(streams_of[5], (NBLK, NP, PTS), 1.0, 6.0, ((0, 8),), jnp.float32)
    return {"records": records, "beam_count": beam_count, "owner_list": owner_list, "block_list": block_list, "travel_table": travel_table, "amp_table": amp_table}


def image_beam(record, travel, amplitude):
    samples = jnp.arange(NS, dtype=jnp.float32)
    weights = jnp.maximum(0.0, 1.0 - jnp.abs(samples[None, :, None] - travel[:, None, :])).astype(jnp.bfloat16)
    weights = lax.optimization_barrier(weights).astype(jnp.float32)
    traces = jnp.einsum('pt,ptx->px', record.reshape(NP, NS).astype(jnp.float32), weights)
    contrib = lax.optimization_barrier(jnp.sum(amplitude * traces, axis=0))
    energy = jnp.mean(jnp.square(record.astype(jnp.float32)))
    lighting = energy * lax.optimization_barrier(jnp.sum(amplitude * amplitude, axis=0))
    return (contrib, lighting)

def reference(records, beam_count, owner_list, block_list, travel_table, amp_table):
    alive_mask = (jnp.arange(BEAM_DEV, dtype=jnp.int32)[None, None, :] < beam_count[:, :, None]).astype(records.dtype)
    live_records = records * alive_mask[None, :, :, :, None]
    padded = jnp.pad(live_records, ((0, 0), (1, 1), (1, 1), (0, 0), (0, 0)))
    sources = jnp.stack([padded[:, 1:-1, 1:-1], padded[:, :-2, 1:-1], padded[:, 2:, 1:-1], padded[:, 1:-1, :-2], padded[:, 1:-1, 2:]], axis=1)
    sources = jnp.transpose(sources, (2, 3, 0, 1, 4, 5)).reshape(N_INLINE * N_XLINE * REQ, NP * NS)
    block_ids = (owner_list[:, 0] * BLK_DEV + block_list[:, 0]).astype(jnp.int32)

    def one_beam(inputs):
        record, block_id = inputs
        return image_beam(record, travel_table[block_id], amp_table[block_id])
    contrib, lighting = lax.map(one_beam, (sources, block_ids), batch_size=16)
    summed = contrib.reshape(N_INLINE, N_XLINE, REQ, PTS).sum(axis=2)
    lighting_sum = lighting.reshape(N_INLINE, N_XLINE, REQ, PTS).sum(axis=2)
    return summed / jnp.sqrt(1.0 + lighting_sum)
```

```python
import functools

import jax
import jax.numpy as jnp
from jax import lax
from jax.experimental import pallas as pl
from jax.experimental.pallas import tpu as pltpu
from jax.sharding import PartitionSpec as P

NS = 128
NP = 64
SOURCES = 5
LISTS = ((0, 0), (0, -1), (0, 1), (1, 0), (-1, 0))


def swap(value, distance):
    members = lax.axis_size("xline")
    return lax.ppermute(value, "xline", [(s, s ^ distance) for s in range(members)])


def gather_blocks(own):
    members = lax.axis_size("xline")
    far = {0: own}
    for distance in range(2, members, 2):
        far[distance] = swap(own, distance)
    out = []
    for distance in range(0, members, 2):
        out += [far[distance], swap(far[distance], 1)]
    return out


def gather_meta(own):
    members = lax.axis_size("xline")
    value, distance = own[None], 1
    while distance < members:
        value = jnp.concatenate([value, swap(value, distance)], axis=0)
        distance *= 2
    return value


def serve_kernel(
    n_tiles, n_shots, n_beams, n_blk, rows, depth,
    place, codes, energy, *refs,
):
    blocks = refs[:n_tiles]
    travel_hbm, amp_hbm, out = refs[n_tiles : n_tiles + 3]
    recs, travel, amp, acc_c, acc_l, todo, rec_sem, sem_t, sem_a = refs[n_tiles + 3 :]
    me_row, me = place[0], place[1]
    per_list = n_shots * n_beams
    count_at = SOURCES * per_list
    for d in range(n_tiles):
        pltpu.make_async_copy(blocks[d], recs.at[d], rec_sem.at[d]).start()
    acc_c[...] = jnp.zeros_like(acc_c)
    acc_l[...] = jnp.zeros_like(acc_l)

    def scan_tile(col, n):
        rel = jnp.bitwise_xor(me, col)
        for m, (drow, dcol) in enumerate(LISTS):
            src = col + dcol
            inside = jnp.logical_and(src >= 0, src < n_tiles)
            src_rel = jnp.bitwise_xor(me, jnp.clip(src, 0, n_tiles - 1))
            count = jnp.where(inside, codes[src_rel, count_at], 0)
            target = jnp.clip(me_row + drow, 0, rows - 1) * n_tiles + col
            for s in range(n_shots):

                def one(b, n, m=m, s=s, rel=rel, src_rel=src_rel, target=target):
                    block = codes[rel, m * per_list + s * n_beams + b] - 1 - me * n_blk
                    todo[0, n] = block
                    todo[1, n] = src_rel
                    todo[2, n] = s * n_beams + b
                    todo[3, n] = target
                    hit = jnp.logical_and(block >= 0, block < n_blk)
                    return n + jnp.where(hit, 1, 0)

                n = lax.fori_loop(0, count, one, n)
        return n

    total = lax.fori_loop(0, n_tiles, scan_tile, jnp.int32(0))

    def copies(q):
        slot = lax.rem(q, depth)
        block = jnp.clip(todo[0, q], 0, n_blk - 1)
        return (
            pltpu.make_async_copy(travel_hbm.at[block], travel.at[slot], sem_t.at[slot]),
            pltpu.make_async_copy(amp_hbm.at[block], amp.at[slot], sem_a.at[slot]),
        )

    def fetch(q):
        for copy in copies(q):
            copy.start()

    def prime(q, carry):
        fetch(q)
        return carry

    lax.fori_loop(0, jnp.minimum(total, depth), prime, 0)
    for d in range(n_tiles):
        pltpu.make_async_copy(blocks[d], recs.at[d], rec_sem.at[d]).wait()

    def work(q, carry):
        slot = lax.rem(q, depth)
        for copy in copies(q):
            copy.wait()
        tile, r, target = todo[1, q], todo[2, q], todo[3, q]
        rec = recs[tile, r].astype(jnp.float32)
        tau, a = travel[slot], amp[slot]
        low = jnp.floor(tau)
        index = low.astype(jnp.int32)
        w0 = jnp.maximum(0.0, 1.0 - jnp.abs(low - tau)).astype(jnp.bfloat16)
        w1 = jnp.maximum(0.0, 1.0 - jnp.abs((low + 1.0) - tau)).astype(jnp.bfloat16)
        r0 = jnp.take_along_axis(rec, index, axis=1, mode="promise_in_bounds")
        r1 = jnp.take_along_axis(rec, index + 1, axis=1, mode="promise_in_bounds")
        traces = r0 * w0.astype(jnp.float32) + r1 * w1.astype(jnp.float32)
        acc_c[target] += jnp.sum((a * traces).reshape(NP // 8, 8, -1), axis=0)
        acc_l[target] += energy[tile, r] * jnp.sum((a * a).reshape(NP // 8, 8, -1), axis=0)

        @pl.when(q + depth < total)
        def _():
            fetch(q + depth)

        return carry

    lax.fori_loop(0, total, work, 0)
    out[:, 0, :] = jnp.sum(acc_c[...], axis=1)
    out[:, 1, :] = jnp.sum(acc_l[...], axis=1)


def serve(place, codes, energy, blocks, travel_table, amp_table, rows):
    n_tiles = len(blocks)
    n_rec = blocks[0].shape[0]
    n_blk, _, points = travel_table.shape
    n_shots = 2
    depth = 16
    any_spec = pl.BlockSpec(memory_space=pl.ANY)
    smem = pl.BlockSpec(memory_space=pltpu.SMEM)
    n_out = rows * n_tiles
    most = SOURCES * n_rec * n_tiles + 1
    return pl.pallas_call(
        functools.partial(serve_kernel, n_tiles, n_shots, n_rec // n_shots, n_blk, rows, depth),
        out_shape=jax.ShapeDtypeStruct((n_out, 2, points), jnp.float32),
        in_specs=[smem] * 3 + [any_spec] * (n_tiles + 2),
        out_specs=pl.BlockSpec(memory_space=pltpu.VMEM),
        scratch_shapes=[
            pltpu.VMEM((n_tiles, n_rec, NP, NS), blocks[0].dtype),
            pltpu.VMEM((depth, NP, points), jnp.float32),
            pltpu.VMEM((depth, NP, points), jnp.float32),
            pltpu.VMEM((n_out, 8, points), jnp.float32),
            pltpu.VMEM((n_out, 8, points), jnp.float32),
            pltpu.SMEM((4, most), jnp.int32),
            pltpu.SemaphoreType.DMA((n_tiles,)),
            pltpu.SemaphoreType.DMA((depth,)),
            pltpu.SemaphoreType.DMA((depth,)),
        ],
    )(place, codes, energy, *blocks, travel_table, amp_table)


def per_device(records, beam_count, owner_list, block_list, travel_table, amp_table):
    rows, members = lax.axis_size("inline"), lax.axis_size("xline")
    me_row, me = lax.axis_index("inline"), lax.axis_index("xline")
    shots, beams = records.shape[0], records.shape[3]
    n_blk = travel_table.shape[0]
    own = records.reshape(shots * beams, NP, NS)
    blocks = gather_blocks(own)

    code = (owner_list[:, 0] * n_blk + block_list[:, 0] + 1).astype(jnp.float32)
    code = code.reshape(shots, SOURCES, beams).transpose(1, 0, 2).reshape(SOURCES, -1)
    down = [(i + 1, i) for i in range(rows - 1)]
    up = [(i, i + 1) for i in range(rows - 1)]
    of_next = lax.ppermute(code[1], "inline", down)
    of_last = lax.ppermute(code[2], "inline", up)
    energy = jnp.mean(jnp.square(own.astype(jnp.float32)), axis=(1, 2))
    meta = jnp.concatenate(
        [code[0], code[3], code[4], of_next, of_last, beam_count[0].astype(jnp.float32), energy]
    )
    meta = gather_meta(meta)
    n_codes = SOURCES * shots * beams + 1
    place = jnp.stack([me_row, me]).astype(jnp.int32)
    sums = serve(
        place,
        meta[:, :n_codes].astype(jnp.int32),
        meta[:, n_codes:],
        blocks,
        travel_table,
        amp_table,
        rows,
    )
    got = lax.all_to_all(sums, ("inline", "xline"), split_axis=0, concat_axis=0, tiled=True)
    got = jnp.sum(got, axis=0)
    return (got[0] / jnp.sqrt(1.0 + got[1]))[None, None, :]


def solution(mesh):
    placed = (
        P(None, "inline", "xline", None, None),
        P("inline", "xline"),
        P(("inline", "xline"), None),
        P(("inline", "xline"), None),
        P("xline", None, None),
        P("xline", None, None),
    )
    return jax.shard_map(
        per_device,
        mesh=mesh,
        in_specs=placed,
        out_specs=P("inline", "xline", None),
        check_vma=False,
    )
```

```python
import functools

import jax
import jax.numpy as jnp
import numpy as np
from jax import lax
from jax.experimental import pallas as pl
from jax.experimental.pallas import tpu as pltpu
from jax.sharding import PartitionSpec as P


NS = 128
NP = 64
SOURCES = 5
UNROLL = 4
LISTS = ((0, 0, 0), (0, 3, 1), (0, 4, -1), (1, 1, 0), (-1, 2, 0))


def swap(value, distance):
    members = lax.axis_size("xline")
    return lax.ppermute(value, "xline", [(s, s ^ distance) for s in range(members)])


def bits(n):
    return max(1, (n - 1).bit_length())


def along_lanes(values, index):
    numbers = lax.GatherDimensionNumbers(
        offset_dims=(),
        collapsed_slice_dims=(1,),
        start_index_map=(1,),
        operand_batching_dims=(0,),
        start_indices_batching_dims=(0,),
    )
    mode = lax.GatherScatterMode.PROMISE_IN_BOUNDS
    return lax.gather(values, index[..., None], numbers, (1, 1), mode=mode)


def plan_kernel(
    n_tiles, n_shots, n_beams, n_blk, rows, groups, place, here, after, before, *refs
):
    n = len(refs) // 2 - 1
    todo, bounds, sems = refs[n], refs[n + 1], refs[-1]
    copies = [pltpu.make_async_copy(refs[i], refs[n + 2 + i], sems.at[i]) for i in range(n)]
    for copy in copies:
        copy.start()
    me_row, me = place[0], place[1]
    per_tile = n_shots * SOURCES * n_beams
    half = n_tiles // 2
    t_bits, b_bits, k_bits = bits(rows * n_tiles + 1), bits(n_beams), bits(n_blk)

    def row_of(rel):
        return lax.shift_right_logical(rel, 1) + half * jnp.bitwise_and(rel, 1)

    def scan_tile(src_rel, n):
        src = jnp.bitwise_xor(me, src_rel)
        count = here[row_of(src_rel), per_tile]
        alive = [lax.shift_right_arithmetic(b - count, 31) for b in range(n_beams)]
        for drow, k, dcol in LISTS:
            lists = {0: here, 1: after, -1: before}[drow]
            mask = alive
            if dcol:
                col = src + dcol
                inside = jnp.where(jnp.logical_and(col >= 0, col < n_tiles), -1, 0)
                col = jnp.clip(col, 0, n_tiles - 1)
                mask = [jnp.bitwise_and(bit, inside) for bit in alive]
                row = row_of(jnp.bitwise_xor(me, col))
            else:
                col, row = src, row_of(src_rel)
            target = jnp.clip(me_row + drow, 0, rows - 1) * n_tiles + col
            first = lax.shift_left(src_rel * n_shots, t_bits + b_bits) + target
            first = lax.shift_left(first, k_bits)
            want = [
                lists[row, (s * SOURCES + k) * n_beams + b]
                for s in range(n_shots)
                for b in range(n_beams)
            ]
            for i, request in enumerate(want):
                request = jnp.bitwise_and(request, mask[i % n_beams])
                todo[n] = request + first
                n = n + lax.shift_right_logical(request, 31)
        return n

    n, low = jnp.int32(0), 0
    bounds[0] = n
    for g, high in enumerate(groups):
        n = lax.fori_loop(low, high, scan_tile, n)
        bounds[g + 1] = n
        low = high
    for copy in copies:
        copy.wait()


def plan(place, lists, n_tiles, n_shots, n_beams, n_blk, rows, groups, arrays):
    smem = pl.BlockSpec(memory_space=pltpu.SMEM)
    vmem = pl.BlockSpec(memory_space=pltpu.VMEM)
    most = SOURCES * n_shots * n_beams * n_tiles + 8
    n = len(arrays)
    return pl.pallas_call(
        functools.partial(plan_kernel, n_tiles, n_shots, n_beams, n_blk, rows, groups),
        out_shape=(
            jax.ShapeDtypeStruct((most,), jnp.int32),
            jax.ShapeDtypeStruct((len(groups) + 1,), jnp.int32),
        )
        + tuple(jax.ShapeDtypeStruct(a.shape, a.dtype) for a in arrays),
        in_specs=[smem] * 4 + [pl.BlockSpec(memory_space=pltpu.HBM)] * n,
        out_specs=(smem, smem) + (vmem,) * n,
        scratch_shapes=[pltpu.SemaphoreType.DMA((n,))],
        cost_estimate=pl.CostEstimate(flops=0, bytes_accessed=12_000_000, transcendentals=0),
        compiler_params=pltpu.CompilerParams(vmem_limit_bytes=24 << 20),
    )(place, *lists, *arrays)


def serve_kernel(group, low, n, n_out, has_prev, todo, bounds, *refs):
    blocks = refs[:n]
    travel, amp = refs[n : n + 2]
    refs = refs[n + 2 :]
    prev = None
    if has_prev:
        prev, refs = refs[0], refs[1:]
    out, recs, energy, acc_c, acc_l = refs
    n_shots, n_beams = blocks[0].shape[:2]
    t_bits, b_bits, k_bits = bits(n_out + 1), bits(n_beams), bits(travel.shape[0])
    first, last = bounds[group], bounds[group + 1]
    acc_c[...] = jnp.zeros_like(acc_c)
    acc_l[...] = jnp.zeros_like(acc_l)
    for d in range(n):

        def spread(s, carry, d=d):
            power = jnp.zeros((n_beams, NS), jnp.float32)
            for p in range(NP):
                part = blocks[d][s, :, p * NS : (p + 1) * NS].astype(jnp.float32)
                recs[d * n_shots + s, pl.ds(p * n_beams, n_beams), :] = part
                power += part * part
            energy[d * n_shots + s] = power
            return carry

        lax.fori_loop(0, n_shots, spread, 0)
    mean = jnp.sum(energy[...], axis=2, keepdims=True) * (1.0 / (NP * NS))
    energy[...] = jnp.broadcast_to(mean, energy.shape)

    def one(q):
        at = jnp.minimum(q, last - 1)
        what = todo[at]
        block = jnp.bitwise_and(what, (1 << k_bits) - 1)
        what = lax.shift_right_logical(jnp.bitwise_and(what, 0x7FFFFFFF), k_bits)
        target = jnp.where(q < last, jnp.bitwise_and(what, (1 << t_bits) - 1), n_out)
        beam = jnp.bitwise_and(lax.shift_right_logical(what, t_bits), (1 << b_bits) - 1)
        row = lax.shift_right_logical(what, t_bits + b_bits) - low * n_shots
        rec = recs[row, pl.ds(beam, NP, stride=n_beams), :]
        level = energy[row, pl.ds(beam, 8, stride=0), :]
        tau, a = travel[block], amp[block]
        low_sample = jnp.floor(tau)
        part = tau - low_sample
        w0 = (1.0 - part).astype(jnp.bfloat16).astype(jnp.float32)
        w1 = part.astype(jnp.bfloat16).astype(jnp.float32)
        index = low_sample.astype(jnp.int32)
        traces = along_lanes(rec, index) * w0 + along_lanes(rec, index + 1) * w1
        contrib = jnp.sum((a * traces).reshape(NP // 8, 8, -1), axis=0)
        light = level * jnp.sum((a * a).reshape(NP // 8, 8, -1), axis=0)
        return target, contrib, light

    def work(i, carry):
        done = [one(first + UNROLL * i + j) for j in range(UNROLL)]
        for target, contrib, light in done:
            acc_c[target] += contrib
            acc_l[target] += light
        return carry

    lax.fori_loop(0, lax.div(last - first + UNROLL - 1, UNROLL), work, 0)
    c = jnp.sum(acc_c[...], axis=1)[:n_out]
    l = jnp.sum(acc_l[...], axis=1)[:n_out]
    if has_prev:
        c, l = c + prev[:, 0, :], l + prev[:, 1, :]
    out[:, 0, :] = c
    out[:, 1, :] = l


def serve(group, low, todo, bounds, blocks, travel_table, amp_table, n_out, prev):
    n = len(blocks)
    shots, beams, _ = blocks[0].shape
    points = travel_table.shape[-1]
    smem = pl.BlockSpec(memory_space=pltpu.SMEM)
    vmem = pl.BlockSpec(memory_space=pltpu.VMEM)
    extra = [] if prev is None else [prev]
    return pl.pallas_call(
        functools.partial(serve_kernel, group, low, n, n_out, prev is not None),
        out_shape=jax.ShapeDtypeStruct((n_out, 2, points), jnp.float32),
        in_specs=[smem] * 2 + [vmem] * (n + 2 + len(extra)),
        out_specs=vmem,
        scratch_shapes=[
            pltpu.VMEM((n * shots, NP * beams, NS), jnp.float32),
            pltpu.VMEM((n * shots, beams, NS), jnp.float32),
            pltpu.VMEM((n_out + 8, 8, points), jnp.float32),
            pltpu.VMEM((n_out + 8, 8, points), jnp.float32),
        ],
        cost_estimate=pl.CostEstimate(flops=0, bytes_accessed=4_000_000 * n, transcendentals=0),
        compiler_params=pltpu.CompilerParams(vmem_limit_bytes=24 << 20),
    )(todo, bounds, *blocks, travel_table, amp_table, *extra)


def per_device(records, beam_count, owner_list, block_list, travel_table, amp_table):
    rows, members = lax.axis_size("inline"), lax.axis_size("xline")
    me_row, me = lax.axis_index("inline"), lax.axis_index("xline")
    shots, beams = records.shape[0], records.shape[3]
    n_blk = travel_table.shape[0]
    outer = range(2, members, 2)

    code = owner_list[:, 0] * n_blk + block_list[:, 0] + 1
    code = jnp.concatenate([code, beam_count[0]])
    lists = [code] + [swap(code, d) for d in outer]

    own = records.reshape(shots, beams, NP * NS)
    far = {0: own}
    for d in outer:
        far[d] = swap(own, d)
    blocks = []
    for d in range(0, members, 2):
        blocks += [far[d], swap(far[d], 1)]

    lists = jnp.stack(lists)
    lists = jnp.concatenate([lists, swap(lists, 1)])
    after = lax.ppermute(lists, "inline", [(i + 1, i) for i in range(rows - 1)])
    before = lax.ppermute(lists, "inline", [(i, i + 1) for i in range(rows - 1)])

    t_bits, b_bits, k_bits = bits(rows * members + 1), bits(beams), bits(n_blk)
    shot, beam = np.divmod(np.arange(shots * SOURCES * beams), SOURCES * beams)
    slot = np.append(shot << b_bits | beam % beams, 0) << (t_bits + k_bits)
    slot = jnp.asarray(slot + np.iinfo(np.int32).min, jnp.int32)
    is_code = jnp.arange(code.shape[0]) < code.shape[0] - 1

    def requests_here(lists):
        block = lists - 1 - me * n_blk
        here = jnp.logical_and(block >= 0, block < n_blk)
        return jnp.where(is_code, jnp.where(here, block + slot, 0), lists)

    place = jnp.stack([me_row, me]).astype(jnp.int32)
    groups = (members // 2, members - 1, members)
    todo, bounds, travel, amp, blocks[0] = plan(
        place, [requests_here(x) for x in (lists, after, before)],
        members, shots, beams, n_blk, rows, groups, tuple(pltpu.with_memory_space_constraint(x, pltpu.HBM) for x in (travel_table, amp_table, own)),
    )
    low, sums = 0, None
    for group, high in enumerate(groups):
        sums = serve(
            group, low, todo, bounds, blocks[low:high], travel, amp,
            rows * members, sums,
        )
        low = high
    got = lax.all_to_all(sums, ("inline", "xline"), split_axis=0, concat_axis=0, tiled=True)
    got = jnp.sum(got, axis=0)
    return (got[0] / jnp.sqrt(1.0 + got[1]))[None, None, :]


def solution(mesh):
    placed = (
        P(None, "inline", "xline", None, None),
        P("inline", "xline"),
        P(("inline", "xline"), None),
        P(("inline", "xline"), None),
        P("xline", None, None),
        P("xline", None, None),
    )
    return jax.shard_map(
        per_device,
        mesh=mesh,
        in_specs=placed,
        out_specs=P("inline", "xline", None),
        check_vma=False,
    )
```
